128 devices in a mesh: scan: 32 (over z, y, core), freq: 4 (over x).
Axes of the slice: x: 4, y: 4, z: 4, core: 2. Of those that a mesh axis runs over, the one named last changes fastest.
Arguments:
- frames: float32 [128, 1024, 512], P('freq', 'scan'), may hold values from -6 to 6
- intersection_masks: int32 [128, 128], replicated, may hold values from -1 to 1
- aperture: int32 [128], replicated, may hold values from 0 to 255
- phases: float32 [256], replicated, may hold values from -3.140625 to 3.140625
Outputs:
- ssb_image: float32 [1024, 2, 512], P(('scan', 'freq'))
The draws below stay inside these ranges and needn't reach their ends.
All inputs are finite; a program needn't handle non-finite values.
Results may differ from the reference program's by a relative error of at most 0.0001.
Values sent between devices are 32-bit elements; how exact they have to be, the bound alone decides.
No kernel may reach another device: no remote copies, remote signals or barrier semaphores. Data moves between devices by JAX's collectives and lax.ppermute only.
A program may use at most 64 MiB of HBM per device.

```python
import math
import jax
import jax.numpy as jnp
from jax import lax

K = 128
SR = 1024
SC = 512
APER = 256
TILES = 128


def plant(drawn, rng, low, high):
    longest = drawn.shape.index(max(drawn.shape))
    spots = []
    for shift in (0, 1):
        where = [jax.random.randint(jax.random.fold_in(rng, axis), (), 0, length) for axis, length in enumerate(drawn.shape)]
        where[longest] = (where[longest] + shift) % drawn.shape[longest]
        spots.append(tuple(where))
    return drawn.at[spots[0]].set(low).at[spots[1]].set(high)


def block_levels(stream_key, dims, split, least, top_value):
    factor_of = 1.0
    for axis_at, parts in split:
        steps = jax.random.uniform(jax.random.fold_in(jax.random.fold_in(stream_key, 6), axis_at), (parts,), jnp.float32, least / len(split), top_value / len(split))
        factor_of = factor_of * jnp.repeat(jnp.exp(steps), dims[axis_at] // parts).reshape((-1,) + (1,) * (len(dims) - 1 - axis_at))
    return factor_of


def scatter_about(own_key, shape, scale, bound, cuts=(), dtype=jnp.bfloat16):
    result = scale * jax.random.normal(own_key, shape, jnp.float32)
    if cuts:
        result = result * block_levels(own_key, shape, cuts, -0.22, 0.18)
    return jnp.clip(result, -bound, bound).astype(dtype)


def setup_inputs(seed: int = 0) -> dict:
    seeds = jax.random.split(jax.random.key(seed), 5)
    frames = scatter_about(seeds[0], (K, SR, SC), 1.0, 6.0, ((0, 4), (1, 32)), jnp.float32)
    intersection_masks = plant(jax.random.randint(seeds[1], (TILES, K), -1, 2), jax.random.fold_in(seeds[1], 1), -1, 1).astype(jnp.int32)
    aperture = plant(jax.random.randint(seeds[2], (K,), 0, APER), jax.random.fold_in(seeds[2], 1), 0, APER - 1).astype(jnp.int32)
    phases = jnp.clip(jax.random.uniform(seeds[3], (APER,), jnp.float32, -3.140625, 3.140625), -3.140625, 3.140625)
    return {"frames": frames, "intersection_masks": intersection_masks, "aperture": aperture, "phases": phases}


def coefficients(intersection_masks, aperture, phases):
    chosen = phases[aperture]
    weight = intersection_masks.astype(jnp.float32)
    return (weight * jnp.cos(chosen)[None, :], weight * jnp.sin(chosen)[None, :])

def reference(frames, intersection_masks, aperture, phases):
    coef_cos, coef_sin = coefficients(intersection_masks, aperture, phases)
    tile_rows = SR // TILES
    rows_cos = jnp.repeat(coef_cos, tile_rows, axis=0).T
    rows_sin = jnp.repeat(coef_sin, tile_rows, axis=0).T

    def accumulate(carry, inputs):
        frame, weight_cos, weight_sin = inputs
        spectrum = jnp.fft.fft2(frame)
        spec_re = jnp.real(spectrum).astype(jnp.float32)
        spec_im = jnp.imag(spectrum).astype(jnp.float32)
        out_re, out_im = carry
        out_re = out_re + weight_cos[:, None] * spec_re + weight_sin[:, None] * spec_im
        out_im = out_im + weight_cos[:, None] * spec_im - weight_sin[:, None] * spec_re
        return ((out_re, out_im), None)
    zeros = jnp.zeros((SR, SC), jnp.float32)
    (out_re, out_im), unused = lax.scan(accumulate, (zeros, zeros), (frames, rows_cos, rows_sin))
    norm_scale = 1.0 / math.sqrt(SR * SC * K)
    return jnp.stack([out_re, out_im], axis=1) * norm_scale
```

```python
import math

import jax
import jax.numpy as jnp
import numpy as np
from jax import lax
from jax.experimental import pallas as pl
from jax.experimental.pallas import tpu as pltpu
from jax.sharding import PartitionSpec as P

AXES = ("scan", "freq")
X0, X1, Y0, Y1, Z0, Z1 = 1, 2, 4, 8, 16, 32
STAGES = (((X0, Y0), (Z0, X1), (Y1, Z1)), ((X1, Z0), (Y0, Z1), (X0, Y1)))


def gray(place):
    return place ^ (place >> 1)


def label_of(device):
    freq, scan = device % 4, device // 4
    core, y, z = scan % 2, scan // 2 % 4, scan // 8
    return (gray(z) << 4) | (gray(y) << 2) | gray(freq), core


def device_of(label, core):
    x, y, z = gray(label & 3), gray(label >> 2 & 3), gray(label >> 4)
    return ((z * 4 + y) * 2 + core) * 4 + x


def flip(core, stage, step):
    low, high = STAGES[core][stage]
    return (step & 1) * low | (step >> 1) * high


def partners(stage, step):
    pairs = []
    for device in range(128):
        label, core = label_of(device)
        pairs.append((device, device_of(label ^ flip(core, stage, step), core)))
    return pairs


def turn(steps):
    quarter = (steps + 128) >> 8
    x = (steps - quarter * 256).astype(jnp.float32) * (2.0 * math.pi / 1024)
    x2 = x * x
    sine = x * (1 + x2 * (-1 / 6 + x2 * (1 / 120 + x2 * (-1 / 5040 + x2 * (1 / 362880)))))
    cosine = 1 + x2 * (-1 / 2 + x2 * (1 / 24 + x2 * (-1 / 720 + x2 * (1 / 40320 - x2 * (1 / 3628800)))))
    swap, minus_c, minus_s = quarter & 1, (quarter + 1) & 2, quarter & 2
    c, s = jnp.where(swap == 1, sine, cosine), jnp.where(swap == 1, cosine, sine)
    return jnp.where(minus_c == 2, -c, c), jnp.where(minus_s == 2, -s, s)


def halves(value):
    high = value.astype(jnp.bfloat16)
    return high, (value - high.astype(jnp.float32)).astype(jnp.bfloat16)


def dot(left, right):
    return jnp.dot(left, right, preferred_element_type=jnp.float32)


def iota(shape, dim):
    return lax.broadcasted_iota(jnp.int32, shape, dim)


def one_hot(hit):
    return jnp.where(hit, 1.0, 0.0).astype(jnp.bfloat16)


def place_of(core, label):
    x, y, z = gray(label & 3), gray(label >> 2 & 3), gray(label >> 4)
    return ((z * 4 + y) * 2 + core) * 4 + x


def fill_matrix(wc, ws, ct, st, high, low):
    tiles = wc.shape[0]
    c, s = ct.reshape(tiles, 8, 128), st.reshape(tiles, 8, 128)
    for at in range(0, wc.shape[1], 128):
        a, b = wc[:, at : at + 128][:, None, :], ws[:, at : at + 128][:, None, :]
        both = jnp.concatenate([a * c - b * s, -(a * s + b * c)], axis=1)
        high[:, at : at + 128], low[:, at : at + 128] = halves(both.reshape(tiles * 16, 128))


def product(a_high, a_low, f_high, f_low):
    return dot(a_high[...], f_high[...]) + dot(a_low[...], f_high[...]) + dot(a_high[...], f_low[...])


def own_kernel(where, frames, masks, aperture, phases, part, wc, ws, ct2, st2, ct, st, a_high, a_low, f_high, f_low):
    scan, freq = where[0], where[1]
    core, y, z = scan & 1, scan >> 1 & 3, scan >> 3
    label = (gray(z) << 4) | (gray(y) << 2) | gray(freq)
    index = iota((64, 128), 0)
    flips = 0
    for stage in range(3):
        for low in range(2):
            bit = jnp.where(core == 0, STAGES[0][stage][low], STAGES[1][stage][low])
            flips = flips + (index >> (4 - 2 * stage + low) & 1) * bit
    tile = place_of(core, label ^ flips)
    lane_pixel = freq * 32 + (iota((128, 1024), 1) >> 5)
    spread = one_hot(iota((128, 1024), 0) == lane_pixel)
    chosen = one_hot(tile == iota((64, 128), 1))
    mask = dot(chosen, masks[...].astype(jnp.float32).astype(jnp.bfloat16)).astype(jnp.bfloat16)
    mask = dot(mask, spread)
    entry = jnp.broadcast_to(aperture[...].astype(jnp.float32), (8, 128)).astype(jnp.bfloat16)
    entry = dot(entry, spread)[:1].astype(jnp.int32)
    pick = one_hot(iota((256, 1024), 0) == entry)
    turns = phases[...]
    parts = []
    for value in (jnp.cos(turns), jnp.sin(turns)):
        for _ in range(3):
            piece = value.astype(jnp.bfloat16).astype(jnp.float32)
            parts.append(piece)
            value = value - piece
    parts = jnp.concatenate(parts + parts[:2], axis=0).astype(jnp.bfloat16)
    picked = dot(parts, pick)
    wc[...] = mask * (picked[0:1] + picked[1:2] + picked[2:3])
    ws[...] = mask * (picked[3:4] + picked[4:5] + picked[5:6])
    for rows, c_out, s_out in ((scan, ct, st), (scan ^ 1, ct2, st2)):
        row = rows * 32 + (iota((64, 128), 1) & 31)
        c1, s1 = turn(tile * 8 * row & 1023)
        row = rows * 32 + (iota((8, 128), 1) & 31)
        c2, s2 = turn(iota((8, 128), 0) * row & 1023)
        c1, s1 = c1[:, None, :], s1[:, None, :]
        c_out[...] = (c1 * c2[None] - s1 * s2[None]).reshape(512, 128)
        s_out[...] = (s1 * c2[None] + c1 * s2[None]).reshape(512, 128)
    f_high[...], f_low[...] = halves(frames[...])

    @pl.loop(0, 4)
    def _(step):
        tiles, rows = pl.ds(pl.multiple_of(step * 16, 16), 16), pl.ds(pl.multiple_of(step * 128, 128), 128)
        fill_matrix(wc[tiles, :], ws[tiles, :], ct[rows, :], st[rows, :], a_high, a_low)
        part[pl.ds(pl.multiple_of(step * 256, 256), 256), :] = product(a_high, a_low, f_high, f_low)


def other_kernel(step, split, frames, part, wc, ws, ct, st, *refs):
    if split:
        out, f_high, f_low, a_high, a_low = refs
        f_high[...], f_low[...] = halves(frames[0][...])
    else:
        out, a_high, a_low = refs
        f_high, f_low = frames
    tiles, rows = slice(step * 16, step * 16 + 16), slice(step * 128, step * 128 + 128)
    fill_matrix(wc[tiles, :], ws[tiles, :], ct[rows, :], st[rows, :], a_high, a_low)
    out[...] = part[step * 256 : step * 256 + 256, :] + product(a_high, a_low, f_high, f_low)


def sum_kernel(a, b, c, d, *outs):
    rows = outs[0].shape[0]
    for step, out in enumerate(outs):
        at = slice(step * rows, step * rows + rows)
        out[...] = a[at, :] + b[at, :] + c[at, :] + d[at, :]


def last_kernel(a, b, c, d, t_high, t_low, out):
    total = a[...] + b[...] + c[...] + d[...]
    columns = total.shape[1]
    high, low = halves(total)
    both = dot(jnp.concatenate([high, low], axis=0), t_high[...])
    both = both[:16] + both[16:] + dot(high, t_low[...])
    out[:, 0, :] = both[:8, :columns] + both[8:, columns:]
    out[:, 1, :] = both[8:, :columns] - both[:8, columns:]


def call(kernel, outs, scratch=(), flops=0, moved=0, inputs=0, limit=40 << 20):
    one = not isinstance(outs, (list, tuple))
    return pl.pallas_call(
        kernel,
        out_shape=outs,
        in_specs=[pl.BlockSpec(memory_space=pltpu.VMEM)] * inputs,
        out_specs=pl.BlockSpec(memory_space=pltpu.VMEM) if one else [pl.BlockSpec(memory_space=pltpu.VMEM)] * len(outs),
        scratch_shapes=list(scratch),
        cost_estimate=pl.CostEstimate(flops=flops, bytes_accessed=moved, transcendentals=0),
        compiler_params=pltpu.CompilerParams(vmem_limit_bytes=limit),
    )


def f32(*shape):
    return jax.ShapeDtypeStruct(shape, jnp.float32)


def bf16(*shape):
    return jax.ShapeDtypeStruct(shape, jnp.bfloat16)


def body(frames, intersection_masks, aperture, phases):
    col_len = frames.shape[2]
    where = jnp.stack([lax.axis_index("scan"), lax.axis_index("freq")]).astype(jnp.int32)
    swap = [(d, (d // 4 ^ 1) * 4 + d % 4) for d in range(128)]
    other = lax.ppermute(frames, AXES, swap).reshape(1024, col_len)
    vmem = pl.BlockSpec(memory_space=pltpu.VMEM)
    part, wc, ws, ct, st = pl.pallas_call(
        own_kernel,
        out_shape=[f32(1024, col_len), f32(64, 1024), f32(64, 1024), f32(512, 128), f32(512, 128)],
        in_specs=[pl.BlockSpec(memory_space=pltpu.SMEM)] + [vmem] * 4,
        out_specs=[vmem] * 5,
        scratch_shapes=[pltpu.VMEM((512, 128), jnp.float32)] * 2
        + [pltpu.VMEM((256, 1024), jnp.bfloat16)] * 2
        + [pltpu.VMEM((1024, col_len), jnp.bfloat16)] * 2,
        cost_estimate=pl.CostEstimate(flops=6 * 1024 * 1024 * 512, bytes_accessed=5 << 20, transcendentals=0),
        compiler_params=pltpu.CompilerParams(vmem_limit_bytes=24 << 20),
    )(where, frames.reshape(1024, col_len), intersection_masks, aperture[None, :], phases[None, :])

    a_scratch = [pltpu.VMEM((256, 1024), jnp.bfloat16)] * 2
    cost = dict(flops=6 * 256 * 1024 * 512, moved=4 << 20)

    def first(step, split, *given):
        outs = [f32(256, col_len)] + ([bf16(1024, col_len)] * 2 if split else [])
        count = len(given)

        def kernel(*refs):
            other_kernel(step, split, refs[:count], *refs[count:])

        return call(kernel, outs, a_scratch, inputs=count + 5, limit=24 << 20, **cost)(*given, part, wc, ws, ct, st)

    send = {}
    send[3], f_high, f_low = first(3, True, other)
    for step in (1, 2, 0):
        (send[step],) = first(step, False, f_high, f_low)
    columns = np.arange(col_len)
    angle = 2.0 * np.pi / col_len * (columns[:, None] * columns[None, :] % col_len)
    scale = 1.0 / math.sqrt(1024 * col_len * 128)
    table = np.concatenate([np.cos(angle), np.sin(angle)], 1) * scale
    t_high = table.astype(jnp.bfloat16)
    t_low = (table - t_high.astype(np.float64)).astype(jnp.bfloat16)
    for stage in range(3):
        got = [lax.ppermute(send[step], AXES, partners(stage, step)) for step in (3, 1, 2)]
        if stage < 2:
            rows = got[0].shape[0] // 4
            send = call(sum_kernel, [f32(rows, col_len)] * 4, inputs=4, moved=rows << 15, limit=8 << 20)(send[0], *got)
    return call(last_kernel, f32(8, 2, col_len), inputs=6, flops=1 << 26, moved=2 << 20, limit=8 << 20)(
        send[0], *got, jnp.asarray(t_high), jnp.asarray(t_low)
    )


def solution(mesh):
    in_specs = (P("freq", "scan", None), P(), P(), P())
    out_specs = P(("scan", "freq"), None, None)
    return jax.shard_map(body, mesh=mesh, in_specs=in_specs, out_specs=out_specs, check_vma=False)
```

```python
import functools
import math

import jax
import jax.numpy as jnp
import numpy as np
from jax import lax
from jax.experimental import pallas as pl
from jax.experimental.pallas import tpu as pltpu
from jax.sharding import PartitionSpec as P

AXES = ("scan", "freq")
X0, X1, Y0, Y1, Z0, Z1 = 1, 2, 4, 8, 16, 32
STAGES = (((X0, Y0), (Z0, X1), (Y1, Z1)), ((X1, Z0), (Y0, Z1), (X0, Y1)))


def gray(place):
    return place ^ (place >> 1)


def label_of(device):
    freq, scan = device % 4, device // 4
    core, y, z = scan % 2, scan // 2 % 4, scan // 8
    return (gray(z) << 4) | (gray(y) << 2) | gray(freq), core


def device_of(label, core):
    x, y, z = gray(label & 3), gray(label >> 2 & 3), gray(label >> 4)
    return ((z * 4 + y) * 2 + core) * 4 + x


def flip(core, stage, step):
    low, high = STAGES[core][stage]
    return (step & 1) * low | (step >> 1) * high


def partners(stage, step):
    pairs = []
    for device in range(128):
        label, core = label_of(device)
        pairs.append((device, device_of(label ^ flip(core, stage, step), core)))
    return pairs


def turn(steps):
    quarter = (steps + 128) >> 8
    x = (steps - quarter * 256).astype(jnp.float32) * (2.0 * math.pi / 1024)
    x2 = x * x
    sine = x * (1 + x2 * (-1 / 6 + x2 * (1 / 120 + x2 * (-1 / 5040 + x2 * (1 / 362880)))))
    cosine = 1 + x2 * (-1 / 2 + x2 * (1 / 24 + x2 * (-1 / 720 + x2 * (1 / 40320 - x2 * (1 / 3628800)))))
    swap, minus_c, minus_s = quarter & 1, (quarter + 1) & 2, quarter & 2
    c, s = jnp.where(swap == 1, sine, cosine), jnp.where(swap == 1, cosine, sine)
    return jnp.where(minus_c == 2, -c, c), jnp.where(minus_s == 2, -s, s)


def halves(value):
    high = value.astype(jnp.bfloat16)
    return high, (value - high.astype(jnp.float32)).astype(jnp.bfloat16)


def dot(left, right):
    return jnp.dot(left, right, preferred_element_type=jnp.float32)


def iota(shape, dim):
    return lax.broadcasted_iota(jnp.int32, shape, dim)


def one_hot(hit):
    return jnp.where(hit, 1.0, 0.0).astype(jnp.bfloat16)


def place_of(core, label):
    x, y, z = gray(label & 3), gray(label >> 2 & 3), gray(label >> 4)
    return ((z * 4 + y) * 2 + core) * 4 + x


def fill_matrix(wc, ws, ct, st, high, low):
    tiles = wc.shape[0]
    c, s = ct.reshape(tiles, 8, 128), st.reshape(tiles, 8, 128)
    for at in range(0, wc.shape[1], 128):
        a, b = wc[:, at : at + 128][:, None, :], ws[:, at : at + 128][:, None, :]
        both = jnp.concatenate([a * c - b * s, -(a * s + b * c)], axis=1)
        high[:, at : at + 128], low[:, at : at + 128] = halves(both.reshape(tiles * 16, 128))


def product(a_high, a_low, f_high, f_low):
    return dot(a_high[...], f_high[...]) + dot(a_low[...], f_high[...]) + dot(a_high[...], f_low[...])


def own_kernel(
    where, frames_in, masks_in, aperture_in, phases_in, part, wc, ws, ct, st, ct2, st2, f_high, f_low,
    frames, masks, aperture, phases, a_high, a_low, sems,
):
    copies = [
        pltpu.make_async_copy(src, dst, sems.at[at])
        for at, (src, dst) in enumerate(
            ((frames_in, frames), (masks_in, masks), (aperture_in, aperture), (phases_in, phases))
        )
    ]
    for copy in copies[1:] + copies[:1]:
        copy.start()
    scan, freq = where[0], where[1]
    core, y, z = scan & 1, scan >> 1 & 3, scan >> 3
    label = (gray(z) << 4) | (gray(y) << 2) | gray(freq)
    index = iota((64, 128), 0)
    flips = 0
    for stage in range(3):
        for low in range(2):
            bit = jnp.where(core == 0, STAGES[0][stage][low], STAGES[1][stage][low])
            flips = flips + (index >> (4 - 2 * stage + low) & 1) * bit
    tile = place_of(core, label ^ flips)
    lane_pixel = freq * 32 + (iota((128, 1024), 1) >> 5)
    spread = one_hot(iota((128, 1024), 0) == lane_pixel)
    chosen = one_hot(tile == iota((64, 128), 1))
    for copy in copies[1:]:
        copy.wait()
    mask = dot(chosen, masks[...].astype(jnp.float32).astype(jnp.bfloat16)).astype(jnp.bfloat16)
    mask = dot(mask, spread)
    entry = jnp.broadcast_to(aperture[...].astype(jnp.float32), (8, 128)).astype(jnp.bfloat16)
    entry = dot(entry, spread)[:1].astype(jnp.int32)
    pick = one_hot(iota((256, 1024), 0) == entry)
    turns = phases[...]
    parts = []
    for value in (jnp.cos(turns), jnp.sin(turns)):
        for _ in range(3):
            piece = value.astype(jnp.bfloat16).astype(jnp.float32)
            parts.append(piece)
            value = value - piece
    parts = jnp.concatenate(parts + parts[:2], axis=0).astype(jnp.bfloat16)
    picked = dot(parts, pick)
    wc[...] = mask * (picked[0:1] + picked[1:2] + picked[2:3])
    ws[...] = mask * (picked[3:4] + picked[4:5] + picked[5:6])
    for rows, c_out, s_out in ((scan, ct, st), (scan ^ 1, ct2, st2)):
        row = rows * 32 + (iota((64, 128), 1) & 31)
        c1, s1 = turn(tile * 8 * row & 1023)
        row = rows * 32 + (iota((8, 128), 1) & 31)
        c2, s2 = turn(iota((8, 128), 0) * row & 1023)
        c1, s1 = c1[:, None, :], s1[:, None, :]
        c_out[...] = (c1 * c2[None] - s1 * s2[None]).reshape(512, 128)
        s_out[...] = (s1 * c2[None] + c1 * s2[None]).reshape(512, 128)
    copies[0].wait()
    f_high[...], f_low[...] = halves(frames[...])

    @pl.loop(1, 4)
    def _(step):
        tiles, rows = pl.ds(pl.multiple_of(step * 16, 16), 16), pl.ds(pl.multiple_of(step * 128, 128), 128)
        fill_matrix(wc[tiles, :], ws[tiles, :], ct[rows, :], st[rows, :], a_high, a_low)
        part[pl.ds(pl.multiple_of(step * 256, 256), 256), :] = product(a_high, a_low, f_high, f_low)


def later_kernel(step, frames, part, wc, ws, ct, st, out, a_high, a_low, f_high, f_low):
    f_high[...], f_low[...] = halves(frames[...])
    tiles, rows = slice(step * 16, step * 16 + 16), slice(step * 128, step * 128 + 128)
    fill_matrix(wc[tiles, :], ws[tiles, :], ct[rows, :], st[rows, :], a_high, a_low)
    out[...] = part[step * 256 : step * 256 + 256, :] + product(a_high, a_low, f_high, f_low)


def near_kernel(own_high, own_low, frames, wc, ws, ct, st, ct2, st2, out, a_high, a_low, f_high, f_low):
    fill_matrix(wc[:16, :], ws[:16, :], ct[:128, :], st[:128, :], a_high, a_low)
    out[...] = product(a_high, a_low, own_high, own_low)
    f_high[...], f_low[...] = halves(frames[...])
    fill_matrix(wc[:16, :], ws[:16, :], ct2[:128, :], st2[:128, :], a_high, a_low)
    out[...] += product(a_high, a_low, f_high, f_low)


def add_kernel(a, b, out):
    out[...] = a[...] + b[...]


def split_kernel(a, b, *outs):
    rows = outs[0].shape[0]
    for step, out in enumerate(outs):
        at = slice(step * rows, step * rows + rows)
        out[...] = a[at, :] + b[at, :]


def sum_kernel(a, b, c, d, *outs):
    rows = outs[0].shape[0]
    for step, out in enumerate(outs):
        at = slice(step * rows, step * rows + rows)
        out[...] = a[at, :] + b[at, :] + c[at, :] + d[at, :]


def last_kernel(a, b, c, d, t_high, t_low, out):
    total = a[...] + b[...] + c[...] + d[...]
    columns = total.shape[1]
    high, low = halves(total)
    both = dot(jnp.concatenate([high, low], axis=0), t_high[...])
    both = both[:16] + both[16:] + dot(high, t_low[...])
    out[:, 0, :] = both[:8, :columns] + both[8:, columns:]
    out[:, 1, :] = both[8:, :columns] - both[:8, columns:]


def call(kernel, outs, scratch=(), flops=0, moved=0, inputs=0, limit=40 << 20):
    one = not isinstance(outs, (list, tuple))
    return pl.pallas_call(
        kernel,
        out_shape=outs,
        in_specs=[pl.BlockSpec(memory_space=pltpu.VMEM)] * inputs,
        out_specs=pl.BlockSpec(memory_space=pltpu.VMEM) if one else [pl.BlockSpec(memory_space=pltpu.VMEM)] * len(outs),
        scratch_shapes=list(scratch),
        cost_estimate=pl.CostEstimate(flops=flops, bytes_accessed=moved, transcendentals=0),
        compiler_params=pltpu.CompilerParams(vmem_limit_bytes=limit),
    )


def f32(*shape):
    return jax.ShapeDtypeStruct(shape, jnp.float32)


def bf16(*shape):
    return jax.ShapeDtypeStruct(shape, jnp.bfloat16)


def body(frames, intersection_masks, aperture, phases):
    col_len = frames.shape[2]
    where = jnp.stack([lax.axis_index("scan"), lax.axis_index("freq")]).astype(jnp.int32)
    swap = [(d, (d // 4 ^ 1) * 4 + d % 4) for d in range(128)]
    other = lax.ppermute(frames, AXES, swap).reshape(1024, col_len)
    vmem = pl.BlockSpec(memory_space=pltpu.VMEM)
    part, wc, ws, ct, st, ct2, st2, f_high, f_low = pl.pallas_call(
        own_kernel,
        out_shape=[f32(1024, col_len)] + [f32(64, 1024)] * 2 + [f32(512, 128)] * 4 + [bf16(1024, col_len)] * 2,
        in_specs=[pl.BlockSpec(memory_space=pltpu.SMEM)] + [pl.BlockSpec(memory_space=pltpu.HBM)] * 4,
        out_specs=[vmem] * 9,
        scratch_shapes=[
            pltpu.VMEM((1024, col_len), jnp.float32),
            pltpu.VMEM((128, 128), jnp.int32),
            pltpu.VMEM((1, 128), jnp.int32),
            pltpu.VMEM((1, 256), jnp.float32),
        ]
        + [pltpu.VMEM((256, 1024), jnp.bfloat16)] * 2
        + [pltpu.SemaphoreType.DMA((4,))],
        cost_estimate=pl.CostEstimate(flops=6 * 768 * 1024 * 512, bytes_accessed=5 << 20, transcendentals=0),
        compiler_params=pltpu.CompilerParams(vmem_limit_bytes=24 << 20),
    )(where, *[pltpu.with_memory_space_constraint(u, pltpu.HBM) for u in (frames.reshape(1024, col_len), intersection_masks, aperture[None, :], phases[None, :])])

    scratch = [pltpu.VMEM((256, 1024), jnp.bfloat16)] * 2 + [pltpu.VMEM((1024, col_len), jnp.bfloat16)] * 2
    cost = dict(flops=1000, moved=1000, limit=24 << 20)
    block = f32(256, col_len)
    send = {
        step: call(functools.partial(later_kernel, step), block, scratch, inputs=6, **cost)(other, part, wc, ws, ct2, st2)
        for step in (3, 1, 2)
    }
    send[0] = call(near_kernel, block, scratch, inputs=9, **cost)(f_high, f_low, other, wc, ws, ct, st, ct2, st2)
    columns = np.arange(col_len)
    angle = 2.0 * np.pi / col_len * (columns[:, None] * columns[None, :] % col_len)
    scale = 1.0 / math.sqrt(1024 * col_len * 128)
    table = np.concatenate([np.cos(angle), np.sin(angle)], 1) * scale
    t_high = table.astype(jnp.bfloat16)
    t_low = (table - t_high.astype(np.float64)).astype(jnp.bfloat16)
    for step in (3, 1):
        got = lax.ppermute(send[step], AXES, partners(0, step))
        send[0] = call(add_kernel, block, inputs=2, moved=3 << 19, limit=8 << 20)(send[0], got)
    got = lax.ppermute(send[2], AXES, partners(0, 2))
    send = call(split_kernel, [f32(64, col_len)] * 4, inputs=2, moved=3 << 19, limit=8 << 20)(send[0], got)
    got = [lax.ppermute(send[step], AXES, partners(1, step)) for step in (3, 1, 2)]
    send = call(sum_kernel, [f32(16, col_len)] * 4, inputs=4, moved=5 << 17, limit=8 << 20)(send[0], *got)
    got = [lax.ppermute(send[step], AXES, partners(2, step)) for step in (3, 1, 2)]
    return call(last_kernel, f32(8, 2, col_len), inputs=6, flops=1 << 26, moved=2 << 20, limit=8 << 20)(
        send[0], *got, jnp.asarray(t_high), jnp.asarray(t_low)
    )


def solution(mesh):
    in_specs = (P("freq", "scan", None), P(), P(), P())
    out_specs = P(("scan", "freq"), None, None)
    return jax.shard_map(body, mesh=mesh, in_specs=in_specs, out_specs=out_specs, check_vma=False)
```

```python
import functools
import math

import jax
import jax.numpy as jnp
import numpy as np
from jax import lax
from jax.experimental import pallas as pl
from jax.experimental.pallas import tpu as pltpu
from jax.sharding import PartitionSpec as P

AXES = ("scan", "freq")
STAGES = (
    ((16, 32, 48), (1, 4, 5), (2, 8, 10)),
    ((1, 2, 3), (16, 32, 48), (4, 8, 12)),
)


def gray(place):
    return place ^ (place >> 1)


def label_of(device):
    freq, scan = device % 4, device // 4
    core, y, z = scan % 2, scan // 2 % 4, scan // 8
    return (gray(z) << 4) | (gray(y) << 2) | gray(freq), core


def device_of(label, core):
    x, y, z = gray(label & 3), gray(label >> 2 & 3), gray(label >> 4)
    return ((z * 4 + y) * 2 + core) * 4 + x


def partners(stage, step):
    pairs = []
    for device in range(128):
        label, core = label_of(device)
        pairs.append((device, device_of(label ^ STAGES[core][stage][step], core)))
    return pairs


def turn(steps):
    quarter = (steps + 128) >> 8
    x = (steps - quarter * 256).astype(jnp.float32) * (2.0 * math.pi / 1024)
    x2 = x * x
    sine = x * (1 + x2 * (-1 / 6 + x2 * (1 / 120 + x2 * (-1 / 5040 + x2 * (1 / 362880)))))
    cosine = 1 + x2 * (-1 / 2 + x2 * (1 / 24 + x2 * (-1 / 720 + x2 * (1 / 40320 - x2 * (1 / 3628800)))))
    swap, minus_c, minus_s = quarter & 1, (quarter + 1) & 2, quarter & 2
    c, s = jnp.where(swap == 1, sine, cosine), jnp.where(swap == 1, cosine, sine)
    return jnp.where(minus_c == 2, -c, c), jnp.where(minus_s == 2, -s, s)


def halves(value):
    high = value.astype(jnp.bfloat16)
    return high, (value - high.astype(jnp.float32)).astype(jnp.bfloat16)


def dot(left, right):
    return jnp.dot(left, right, preferred_element_type=jnp.float32)


def iota(shape, dim):
    return lax.broadcasted_iota(jnp.int32, shape, dim)


def one_hot(hit):
    return jnp.where(hit, 1.0, 0.0).astype(jnp.bfloat16)


def place_of(core, label):
    x, y, z = gray(label & 3), gray(label >> 2 & 3), gray(label >> 4)
    return ((z * 4 + y) * 2 + core) * 4 + x


def fill_matrix(wc, ws, ct, st, high, low):
    tiles = wc.shape[0]
    c, s = ct.reshape(tiles, 8, 128), st.reshape(tiles, 8, 128)
    for at in range(0, wc.shape[1], 128):
        a, b = wc[:, at : at + 128][:, None, :], ws[:, at : at + 128][:, None, :]
        both = jnp.concatenate([a * c - b * s, -(a * s + b * c)], axis=1)
        high[:, at : at + 128], low[:, at : at + 128] = halves(both.reshape(tiles * 16, 128))


def product(a_high, a_low, f_high, f_low):
    return dot(a_high[...], f_high[...]) + dot(a_low[...], f_high[...]) + dot(a_high[...], f_low[...])


def own_kernel(
    where, frames_in, masks_in, aperture_in, phases_in, part, wc, ws, ct, st, ct2, st2, f_high, f_low,
    frames, masks, aperture, phases, a_high, a_low, sems,
):
    pieces = [pl.ds(at * 128, 128) for at in range(8)]
    pairs = [(masks_in, masks), (aperture_in, aperture), (phases_in, phases)]
    pairs += [(frames_in.at[piece, :], frames.at[piece, :]) for piece in pieces]
    copies = [pltpu.make_async_copy(src, dst, sems.at[at]) for at, (src, dst) in enumerate(pairs)]
    for copy in copies:
        copy.start()
    scan, freq = where[0], where[1]
    core, y, z = scan & 1, scan >> 1 & 3, scan >> 3
    label = (gray(z) << 4) | (gray(y) << 2) | gray(freq)
    index = iota((64, 128), 0)
    flips = jnp.zeros_like(index)
    for stage in range(3):
        digit = index >> (4 - 2 * stage) & 3
        for step in range(3):
            flip = jnp.where(core == 0, STAGES[0][stage][step], STAGES[1][stage][step])
            flips = flips ^ jnp.where(digit == step + 1, flip, 0)
    tile = place_of(core, label ^ flips)
    lane_pixel = freq * 32 + (iota((128, 1024), 1) >> 5)
    spread = one_hot(iota((128, 1024), 0) == lane_pixel)
    chosen = one_hot(tile == iota((64, 128), 1))
    for copy in copies[:3]:
        copy.wait()
    mask = dot(chosen, masks[...].astype(jnp.float32).astype(jnp.bfloat16)).astype(jnp.bfloat16)
    mask = dot(mask, spread)
    entry = jnp.broadcast_to(aperture[...].astype(jnp.float32), (8, 128)).astype(jnp.bfloat16)
    entry = dot(entry, spread)[:1].astype(jnp.int32)
    pick = one_hot(iota((256, 1024), 0) == entry)
    turns = phases[...]
    parts = []
    for value in (jnp.cos(turns), jnp.sin(turns)):
        for _ in range(3):
            piece = value.astype(jnp.bfloat16).astype(jnp.float32)
            parts.append(piece)
            value = value - piece
    parts = jnp.concatenate(parts + parts[:2], axis=0).astype(jnp.bfloat16)
    picked = dot(parts, pick)
    wc[...] = mask * (picked[0:1] + picked[1:2] + picked[2:3])
    ws[...] = mask * (picked[3:4] + picked[4:5] + picked[5:6])
    for rows, c_out, s_out in ((scan, ct, st), (scan ^ 1, ct2, st2)):
        row = rows * 32 + (iota((64, 128), 1) & 31)
        c1, s1 = turn(tile * 8 * row & 1023)
        row = rows * 32 + (iota((8, 128), 1) & 31)
        c2, s2 = turn(iota((8, 128), 0) * row & 1023)
        c1, s1 = c1[:, None, :], s1[:, None, :]
        c_out[...] = (c1 * c2[None] - s1 * s2[None]).reshape(512, 128)
        s_out[...] = (s1 * c2[None] + c1 * s2[None]).reshape(512, 128)
    for piece, copy in zip(pieces, copies[3:]):
        copy.wait()
        f_high[piece, :], f_low[piece, :] = halves(frames[piece, :])
    for step in (1, 2, 3):
        tiles, rows = slice(step * 16, step * 16 + 16), slice(step * 128, step * 128 + 128)
        high, low = a_high.at[step - 1], a_low.at[step - 1]
        fill_matrix(wc[tiles, :], ws[tiles, :], ct[rows, :], st[rows, :], high, low)
        part[step * 256 : step * 256 + 256, :] = product(high, low, f_high, f_low)


def later_kernel(step, frames, part, wc, ws, ct, st, out, a_high, a_low, f_high, f_low):
    f_high[...], f_low[...] = halves(frames[...])
    tiles, rows = slice(step * 16, step * 16 + 16), slice(step * 128, step * 128 + 128)
    fill_matrix(wc[tiles, :], ws[tiles, :], ct[rows, :], st[rows, :], a_high, a_low)
    out[...] = part[step * 256 : step * 256 + 256, :] + product(a_high, a_low, f_high, f_low)


def near_kernel(own_high, own_low, frames, wc, ws, ct, st, ct2, st2, out, a_high, a_low, f_high, f_low):
    fill_matrix(wc[:16, :], ws[:16, :], ct[:128, :], st[:128, :], a_high, a_low)
    out[...] = product(a_high, a_low, own_high, own_low)
    f_high[...], f_low[...] = halves(frames[...])
    fill_matrix(wc[:16, :], ws[:16, :], ct2[:128, :], st2[:128, :], a_high, a_low)
    out[...] += product(a_high, a_low, f_high, f_low)


def add_kernel(a, b, out):
    out[...] = a[...] + b[...]


def split_kernel(a, b, *outs):
    rows = outs[0].shape[0]
    for step, out in enumerate(outs):
        at = slice(step * rows, step * rows + rows)
        out[...] = a[at, :] + b[at, :]


def sum_kernel(a, b, c, d, *outs):
    rows = outs[0].shape[0]
    for step, out in enumerate(outs):
        at = slice(step * rows, step * rows + rows)
        out[...] = a[at, :] + b[at, :] + c[at, :] + d[at, :]


def last_kernel(a, b, c, d, t_high, t_low, out):
    total = a[...] + b[...] + c[...] + d[...]
    columns = total.shape[1]
    high, low = halves(total)
    both = dot(jnp.concatenate([high, low], axis=0), t_high[...])
    both = both[:16] + both[16:] + dot(high, t_low[...])
    out[:, 0, :] = both[:8, :columns] + both[8:, columns:]
    out[:, 1, :] = both[8:, :columns] - both[:8, columns:]


def call(kernel, outs, scratch=(), flops=0, moved=0, inputs=0, limit=40 << 20):
    one = not isinstance(outs, (list, tuple))
    return pl.pallas_call(
        kernel,
        out_shape=outs,
        in_specs=[pl.BlockSpec(memory_space=pltpu.VMEM)] * inputs,
        out_specs=pl.BlockSpec(memory_space=pltpu.VMEM) if one else [pl.BlockSpec(memory_space=pltpu.VMEM)] * len(outs),
        scratch_shapes=list(scratch),
        cost_estimate=pl.CostEstimate(flops=flops, bytes_accessed=moved, transcendentals=0),
        compiler_params=pltpu.CompilerParams(vmem_limit_bytes=limit),
    )


def f32(*shape):
    return jax.ShapeDtypeStruct(shape, jnp.float32)


def bf16(*shape):
    return jax.ShapeDtypeStruct(shape, jnp.bfloat16)


def body(frames, intersection_masks, aperture, phases):
    col_len = frames.shape[2]
    where = jnp.stack([lax.axis_index("scan"), lax.axis_index("freq")]).astype(jnp.int32)
    swap = [(d, (d // 4 ^ 1) * 4 + d % 4) for d in range(128)]
    other = lax.ppermute(frames, AXES, swap).reshape(1024, col_len)
    vmem = pl.BlockSpec(memory_space=pltpu.VMEM)
    part, wc, ws, ct, st, ct2, st2, f_high, f_low = pl.pallas_call(
        own_kernel,
        out_shape=[f32(1024, col_len)] + [f32(64, 1024)] * 2 + [f32(512, 128)] * 4 + [bf16(1024, col_len)] * 2,
        in_specs=[pl.BlockSpec(memory_space=pltpu.SMEM)] + [pl.BlockSpec(memory_space=pltpu.HBM)] * 4,
        out_specs=[vmem] * 9,
        scratch_shapes=[
            pltpu.VMEM((1024, col_len), jnp.float32),
            pltpu.VMEM((128, 128), jnp.int32),
            pltpu.VMEM((1, 128), jnp.int32),
            pltpu.VMEM((1, 256), jnp.float32),
        ]
        + [pltpu.VMEM((3, 256, 1024), jnp.bfloat16)] * 2
        + [pltpu.SemaphoreType.DMA((11,))],
        cost_estimate=pl.CostEstimate(flops=6 * 768 * 1024 * 512, bytes_accessed=5 << 20, transcendentals=0),
        compiler_params=pltpu.CompilerParams(vmem_limit_bytes=24 << 20),
    )(where, *[pltpu.with_memory_space_constraint(u, pltpu.HBM) for u in (frames.reshape(1024, col_len), intersection_masks, aperture[None, :], phases[None, :])])

    scratch = [pltpu.VMEM((256, 1024), jnp.bfloat16)] * 2 + [pltpu.VMEM((1024, col_len), jnp.bfloat16)] * 2
    cost = dict(flops=1000, moved=1000, limit=24 << 20)
    block = f32(256, col_len)
    send = {
        step: call(functools.partial(later_kernel, step), block, scratch, inputs=6, **cost)(other, part, wc, ws, ct2, st2)
        for step in (3, 1, 2)
    }
    send[0] = call(near_kernel, block, scratch, inputs=9, **cost)(f_high, f_low, other, wc, ws, ct, st, ct2, st2)
    columns = np.arange(col_len)
    angle = 2.0 * np.pi / col_len * (columns[:, None] * columns[None, :] % col_len)
    scale = 1.0 / math.sqrt(1024 * col_len * 128)
    table = np.concatenate([np.cos(angle), np.sin(angle)], 1) * scale
    t_high = table.astype(jnp.bfloat16)
    t_low = (table - t_high.astype(np.float64)).astype(jnp.bfloat16)
    for step in (3, 1):
        got = lax.ppermute(send[step], AXES, partners(0, step - 1))
        send[0] = call(add_kernel, block, inputs=2, moved=3 << 19, limit=8 << 20)(send[0], got)
    got = lax.ppermute(send[2], AXES, partners(0, 1))
    send = call(split_kernel, [f32(64, col_len)] * 4, inputs=2, moved=3 << 19, limit=8 << 20)(send[0], got)
    got = [lax.ppermute(send[step], AXES, partners(1, step - 1)) for step in (3, 1, 2)]
    send = call(sum_kernel, [f32(16, col_len)] * 4, inputs=4, moved=5 << 17, limit=8 << 20)(send[0], *got)
    got = [lax.ppermute(send[step], AXES, partners(2, step - 1)) for step in (3, 1, 2)]
    return call(last_kernel, f32(8, 2, col_len), inputs=6, flops=1 << 26, moved=2 << 20, limit=8 << 20)(
        send[0], *got, jnp.asarray(t_high), jnp.asarray(t_low)
    )


def solution(mesh):
    in_specs = (P("freq", "scan", None), P(), P(), P())
    out_specs = P(("scan", "freq"), None, None)
    return jax.shard_map(body, mesh=mesh, in_specs=in_specs, out_specs=out_specs, check_vma=False)
```

```python
import functools
import math

import jax
import jax.numpy as jnp
import numpy as np
from jax import lax
from jax.experimental import pallas as pl
from jax.experimental.pallas import tpu as pltpu
from jax.sharding import PartitionSpec as P

AXES = ("scan", "freq")
STAGES = (
    ((16, 32, 48), (2, 8, 10), (1, 4, 5)),
    ((1, 2, 3), (16, 32, 48), (4, 8, 12)),
)


def gray(place):
    return place ^ (place >> 1)


def label_of(device):
    freq, scan = device % 4, device // 4
    core, y, z = scan % 2, scan // 2 % 4, scan // 8
    return (gray(z) << 4) | (gray(y) << 2) | gray(freq), core


def device_of(label, core):
    x, y, z = gray(label & 3), gray(label >> 2 & 3), gray(label >> 4)
    return ((z * 4 + y) * 2 + core) * 4 + x


def partners(stage, step):
    pairs = []
    for device in range(128):
        label, core = label_of(device)
        pairs.append((device, device_of(label ^ STAGES[core][stage][step], core)))
    return pairs


def turn(steps):
    quarter = (steps + 128) >> 8
    x = (steps - quarter * 256).astype(jnp.float32) * (2.0 * math.pi / 1024)
    x2 = x * x
    sine = x * (1 + x2 * (-1 / 6 + x2 * (1 / 120 + x2 * (-1 / 5040 + x2 * (1 / 362880)))))
    cosine = 1 + x2 * (-1 / 2 + x2 * (1 / 24 + x2 * (-1 / 720 + x2 * (1 / 40320 - x2 * (1 / 3628800)))))
    swap, minus_c, minus_s = quarter & 1, (quarter + 1) & 2, quarter & 2
    c, s = jnp.where(swap == 1, sine, cosine), jnp.where(swap == 1, cosine, sine)
    return jnp.where(minus_c == 2, -c, c), jnp.where(minus_s == 2, -s, s)


def halves(value):
    high = value.astype(jnp.bfloat16)
    return high, (value - high.astype(jnp.float32)).astype(jnp.bfloat16)


def dot(left, right):
    return jnp.dot(left, right, preferred_element_type=jnp.float32)


def iota(shape, dim):
    return lax.broadcasted_iota(jnp.int32, shape, dim)


def one_hot(hit):
    return jnp.where(hit, 1.0, 0.0).astype(jnp.bfloat16)


def place_of(core, label):
    x, y, z = gray(label & 3), gray(label >> 2 & 3), gray(label >> 4)
    return ((z * 4 + y) * 2 + core) * 4 + x


def fill_matrix(wc, ws, ct, st, high, low):
    tiles = wc.shape[0]
    c, s = ct.reshape(tiles, 8, 128), st.reshape(tiles, 8, 128)
    for at in range(0, wc.shape[1], 128):
        a, b = wc[:, at : at + 128][:, None, :], ws[:, at : at + 128][:, None, :]
        both = jnp.concatenate([a * c - b * s, -(a * s + b * c)], axis=1)
        high[:, at : at + 128], low[:, at : at + 128] = halves(both.reshape(tiles * 16, 128))


def product(a_high, a_low, f_high, f_low):
    return dot(a_high[...], f_high[...]) + dot(a_low[...], f_high[...]) + dot(a_high[...], f_low[...])


def own_kernel(
    where, frames_in, masks_in, aperture_in, phases_in, part, wc, ws, ct, st, ct2, st2, f_high, f_low,
    frames, masks, aperture, phases, a_high, a_low, sems,
):
    pieces = [pl.ds(at * 128, 128) for at in range(8)]
    pairs = [(masks_in, masks), (aperture_in, aperture), (phases_in, phases)]
    pairs += [(frames_in.at[piece, :], frames.at[piece, :]) for piece in pieces]
    copies = [pltpu.make_async_copy(src, dst, sems.at[at]) for at, (src, dst) in enumerate(pairs)]
    for copy in copies:
        copy.start()
    scan, freq = where[0], where[1]
    core, y, z = scan & 1, scan >> 1 & 3, scan >> 3
    label = (gray(z) << 4) | (gray(y) << 2) | gray(freq)
    index = iota((64, 128), 0)
    flips = jnp.zeros_like(index)
    for stage in range(3):
        digit = index >> (4 - 2 * stage) & 3
        for step in range(3):
            flip = jnp.where(core == 0, STAGES[0][stage][step], STAGES[1][stage][step])
            flips = flips ^ jnp.where(digit == step + 1, flip, 0)
    tile = place_of(core, label ^ flips)
    lane_pixel = freq * 32 + (iota((128, 1024), 1) >> 5)
    spread = one_hot(iota((128, 1024), 0) == lane_pixel)
    chosen = one_hot(tile == iota((64, 128), 1))
    for copy in copies[:3]:
        copy.wait()
    mask = dot(chosen, masks[...].astype(jnp.float32).astype(jnp.bfloat16)).astype(jnp.bfloat16)
    mask = dot(mask, spread)
    entry = jnp.broadcast_to(aperture[...].astype(jnp.float32), (8, 128)).astype(jnp.bfloat16)
    entry = dot(entry, spread)[:1].astype(jnp.int32)
    pick = one_hot(iota((256, 1024), 0) == entry)
    turns = phases[...]
    parts = []
    for value in (jnp.cos(turns), jnp.sin(turns)):
        for _ in range(3):
            piece = value.astype(jnp.bfloat16).astype(jnp.float32)
            parts.append(piece)
            value = value - piece
    parts = jnp.concatenate(parts + parts[:2], axis=0).astype(jnp.bfloat16)
    picked = dot(parts, pick)
    wc[...] = mask * (picked[0:1] + picked[1:2] + picked[2:3])
    ws[...] = mask * (picked[3:4] + picked[4:5] + picked[5:6])
    for rows, c_out, s_out in ((scan, ct, st), (scan ^ 1, ct2, st2)):
        row = rows * 32 + (iota((64, 128), 1) & 31)
        c1, s1 = turn(tile * 8 * row & 1023)
        row = rows * 32 + (iota((8, 128), 1) & 31)
        c2, s2 = turn(iota((8, 128), 0) * row & 1023)
        c1, s1 = c1[:, None, :], s1[:, None, :]
        c_out[...] = (c1 * c2[None] - s1 * s2[None]).reshape(512, 128)
        s_out[...] = (s1 * c2[None] + c1 * s2[None]).reshape(512, 128)
    for piece, copy in zip(pieces, copies[3:]):
        copy.wait()
        f_high[piece, :], f_low[piece, :] = halves(frames[piece, :])
    for step in (1, 2, 3):
        tiles, rows = slice(step * 16, step * 16 + 16), slice(step * 128, step * 128 + 128)
        high, low = a_high.at[step - 1], a_low.at[step - 1]
        fill_matrix(wc[tiles, :], ws[tiles, :], ct[rows, :], st[rows, :], high, low)
        part[step * 256 : step * 256 + 256, :] = product(high, low, f_high, f_low)


def later_kernel(step, frames, part, wc, ws, ct, st, out, a_high, a_low, f_high, f_low):
    f_high[...], f_low[...] = halves(frames[...])
    tiles, rows = slice(step * 16, step * 16 + 16), slice(step * 128, step * 128 + 128)
    fill_matrix(wc[tiles, :], ws[tiles, :], ct[rows, :], st[rows, :], a_high, a_low)
    out[...] = part[step * 256 : step * 256 + 256, :] + product(a_high, a_low, f_high, f_low)


def near_kernel(own_high, own_low, frames, wc, ws, ct, st, ct2, st2, out, a_high, a_low, f_high, f_low):
    fill_matrix(wc[:16, :], ws[:16, :], ct[:128, :], st[:128, :], a_high, a_low)
    out[...] = product(a_high, a_low, own_high, own_low)
    f_high[...], f_low[...] = halves(frames[...])
    fill_matrix(wc[:16, :], ws[:16, :], ct2[:128, :], st2[:128, :], a_high, a_low)
    out[...] += product(a_high, a_low, f_high, f_low)


def add_kernel(a, b, out):
    out[...] = a[...] + b[...]


def split_kernel(a, b, *outs):
    rows = outs[0].shape[0]
    for step, out in enumerate(outs):
        at = slice(step * rows, step * rows + rows)
        out[...] = a[at, :] + b[at, :]


def sum_kernel(a, b, c, d, *outs):
    rows = outs[0].shape[0]
    for step, out in enumerate(outs):
        at = slice(step * rows, step * rows + rows)
        out[...] = a[at, :] + b[at, :] + c[at, :] + d[at, :]


def last_kernel(a, b, c, d, t_high, t_low, out):
    total = a[...] + b[...] + c[...] + d[...]
    columns = total.shape[1]
    high, low = halves(total)
    both = dot(jnp.concatenate([high, low], axis=0), t_high[...])
    both = both[:16] + both[16:] + dot(high, t_low[...])
    out[:, 0, :] = both[:8, :columns] + both[8:, columns:]
    out[:, 1, :] = both[8:, :columns] - both[:8, columns:]


def call(kernel, outs, scratch=(), flops=0, moved=0, inputs=0, limit=40 << 20):
    one = not isinstance(outs, (list, tuple))
    return pl.pallas_call(
        kernel,
        out_shape=outs,
        in_specs=[pl.BlockSpec(memory_space=pltpu.VMEM)] * inputs,
        out_specs=pl.BlockSpec(memory_space=pltpu.VMEM) if one else [pl.BlockSpec(memory_space=pltpu.VMEM)] * len(outs),
        scratch_shapes=list(scratch),
        cost_estimate=pl.CostEstimate(flops=flops, bytes_accessed=moved, transcendentals=0),
        compiler_params=pltpu.CompilerParams(vmem_limit_bytes=limit),
    )


def f32(*shape):
    return jax.ShapeDtypeStruct(shape, jnp.float32)


def bf16(*shape):
    return jax.ShapeDtypeStruct(shape, jnp.bfloat16)


def body(frames, intersection_masks, aperture, phases):
    col_len = frames.shape[2]
    where = jnp.stack([lax.axis_index("scan"), lax.axis_index("freq")]).astype(jnp.int32)
    swap = [(d, (d // 4 ^ 1) * 4 + d % 4) for d in range(128)]
    other = lax.ppermute(frames, AXES, swap).reshape(1024, col_len)
    vmem = pl.BlockSpec(memory_space=pltpu.VMEM)
    part, wc, ws, ct, st, ct2, st2, f_high, f_low = pl.pallas_call(
        own_kernel,
        out_shape=[f32(1024, col_len)] + [f32(64, 1024)] * 2 + [f32(512, 128)] * 4 + [bf16(1024, col_len)] * 2,
        in_specs=[pl.BlockSpec(memory_space=pltpu.SMEM)] + [pl.BlockSpec(memory_space=pltpu.HBM)] * 4,
        out_specs=[vmem] * 9,
        scratch_shapes=[
            pltpu.VMEM((1024, col_len), jnp.float32),
            pltpu.VMEM((128, 128), jnp.int32),
            pltpu.VMEM((1, 128), jnp.int32),
            pltpu.VMEM((1, 256), jnp.float32),
        ]
        + [pltpu.VMEM((3, 256, 1024), jnp.bfloat16)] * 2
        + [pltpu.SemaphoreType.DMA((11,))],
        cost_estimate=pl.CostEstimate(flops=6 * 768 * 1024 * 512, bytes_accessed=5 << 20, transcendentals=0),
        compiler_params=pltpu.CompilerParams(vmem_limit_bytes=24 << 20),
    )(where, *[pltpu.with_memory_space_constraint(u, pltpu.HBM) for u in (frames.reshape(1024, col_len), intersection_masks, aperture[None, :], phases[None, :])])

    scratch = [pltpu.VMEM((256, 1024), jnp.bfloat16)] * 2 + [pltpu.VMEM((1024, col_len), jnp.bfloat16)] * 2
    cost = dict(flops=1000, moved=1000, limit=24 << 20)
    block = f32(256, col_len)
    send = {
        step: call(functools.partial(later_kernel, step), block, scratch, inputs=6, **cost)(other, part, wc, ws, ct2, st2)
        for step in (3, 2, 1)
    }
    send[0] = call(near_kernel, block, scratch, inputs=9, **cost)(f_high, f_low, other, wc, ws, ct, st, ct2, st2)
    columns = np.arange(col_len)
    angle = 2.0 * np.pi / col_len * (columns[:, None] * columns[None, :] % col_len)
    scale = 1.0 / math.sqrt(1024 * col_len * 128)
    table = np.concatenate([np.cos(angle), np.sin(angle)], 1) * scale
    t_high = table.astype(jnp.bfloat16)
    t_low = (table - t_high.astype(np.float64)).astype(jnp.bfloat16)
    for step in (3, 2):
        got = lax.ppermute(send[step], AXES, partners(0, step - 1))
        send[0] = call(add_kernel, block, inputs=2, moved=3 << 19, limit=8 << 20)(send[0], got)
    got = lax.ppermute(send[1], AXES, partners(0, 0))
    send = call(split_kernel, [f32(64, col_len)] * 4, inputs=2, moved=3 << 19, limit=8 << 20)(send[0], got)
    got = [lax.ppermute(send[step], AXES, partners(1, step - 1)) for step in (3, 2, 1)]
    send = call(sum_kernel, [f32(16, col_len)] * 4, inputs=4, moved=5 << 17, limit=8 << 20)(send[0], *got)
    got = [lax.ppermute(send[step], AXES, partners(2, step - 1)) for step in (3, 2, 1)]
    return call(last_kernel, f32(8, 2, col_len), inputs=6, flops=1 << 26, moved=2 << 20, limit=8 << 20)(
        send[0], *got, jnp.asarray(t_high), jnp.asarray(t_low)
    )


def solution(mesh):
    in_specs = (P("freq", "scan", None), P(), P(), P())
    out_specs = P(("scan", "freq"), None, None)
    return jax.shard_map(body, mesh=mesh, in_specs=in_specs, out_specs=out_specs, check_vma=False)
```

```python
import functools
import math

import jax
import jax.numpy as jnp
import numpy as np
from jax import lax
from jax.experimental import pallas as pl
from jax.experimental.pallas import tpu as pltpu
from jax.sharding import PartitionSpec as P

AXES = ("scan", "freq")
STAGES = (
    ((16, 32, 48), (2, 8, 10), (1, 4, 5)),
    ((1, 2, 3), (16, 32, 48), (4, 8, 12)),
)


def gray(place):
    return place ^ (place >> 1)


def label_of(device):
    freq, scan = device % 4, device // 4
    core, y, z = scan % 2, scan // 2 % 4, scan // 8
    return (gray(z) << 4) | (gray(y) << 2) | gray(freq), core


def device_of(label, core):
    x, y, z = gray(label & 3), gray(label >> 2 & 3), gray(label >> 4)
    return ((z * 4 + y) * 2 + core) * 4 + x


def partners(stage, step):
    pairs = []
    for device in range(128):
        label, core = label_of(device)
        pairs.append((device, device_of(label ^ STAGES[core][stage][step], core)))
    return pairs


def turn(steps):
    quarter = (steps + 128) >> 8
    x = (steps - quarter * 256).astype(jnp.float32) * (2.0 * math.pi / 1024)
    x2 = x * x
    sine = x * (1 + x2 * (-1 / 6 + x2 * (1 / 120 + x2 * (-1 / 5040 + x2 * (1 / 362880)))))
    cosine = 1 + x2 * (-1 / 2 + x2 * (1 / 24 + x2 * (-1 / 720 + x2 * (1 / 40320 - x2 * (1 / 3628800)))))
    swap, minus_c, minus_s = quarter & 1, (quarter + 1) & 2, quarter & 2
    c, s = jnp.where(swap == 1, sine, cosine), jnp.where(swap == 1, cosine, sine)
    return jnp.where(minus_c == 2, -c, c), jnp.where(minus_s == 2, -s, s)


def halves(value):
    high = value.astype(jnp.bfloat16)
    return high, (value - high.astype(jnp.float32)).astype(jnp.bfloat16)


def dot(left, right):
    return jnp.dot(left, right, preferred_element_type=jnp.float32)


def iota(shape, dim):
    return lax.broadcasted_iota(jnp.int32, shape, dim)


def one_hot(hit):
    return jnp.where(hit, 1.0, 0.0).astype(jnp.bfloat16)


def place_of(core, label):
    x, y, z = gray(label & 3), gray(label >> 2 & 3), gray(label >> 4)
    return ((z * 4 + y) * 2 + core) * 4 + x


def fill_matrix(wc, ws, ct, st, high, low):
    tiles = wc.shape[0]
    c, s = ct.reshape(tiles, 8, 128), st.reshape(tiles, 8, 128)
    for at in range(0, wc.shape[1], 128):
        a, b = wc[:, at : at + 128][:, None, :], ws[:, at : at + 128][:, None, :]
        both = jnp.concatenate([a * c + b * s, a * s - b * c], axis=1)
        high[:, at : at + 128], low[:, at : at + 128] = halves(both.reshape(tiles * 16, 128))


def product(a_high, a_low, f_high, f_low):
    return dot(a_high[...], f_high[...]) + dot(a_low[...], f_high[...]) + dot(a_high[...], f_low[...])


def own_kernel(
    where, frames_in, masks_in, aperture_in, phases_in, part, wc, ws, ct, st, ct2, st2, f_high, f_low,
    frames, masks, aperture, phases, sems, *matrices,
):
    pieces = [pl.ds(at * 128, 128) for at in range(8)]
    pairs = [(masks_in, masks), (aperture_in, aperture), (phases_in, phases)]
    pairs += [(frames_in.at[piece, :], frames.at[piece, :]) for piece in pieces]
    copies = [pltpu.make_async_copy(src, dst, sems.at[at]) for at, (src, dst) in enumerate(pairs)]
    for copy in copies:
        copy.start()
    scan, freq = where[0], where[1]
    core, y, z = scan & 1, scan >> 1 & 3, scan >> 3
    label = (gray(z) << 4) | (gray(y) << 2) | gray(freq)
    index = iota((64, 128), 0)
    flips = jnp.zeros_like(index)
    for stage in range(3):
        digit = index >> (4 - 2 * stage) & 3
        for step in range(3):
            flip = jnp.where(core == 0, STAGES[0][stage][step], STAGES[1][stage][step])
            flips = flips ^ jnp.where(digit == step + 1, flip, 0)
    tile = place_of(core, label ^ flips)
    lane_pixel = freq * 32 + (iota((128, 1024), 1) >> 5)
    spread = one_hot(iota((128, 1024), 0) == lane_pixel)
    chosen = one_hot(tile == iota((64, 128), 1))
    for copy in copies[:3]:
        copy.wait()
    mask = dot(chosen, masks[...].astype(jnp.float32).astype(jnp.bfloat16)).astype(jnp.bfloat16)
    mask = dot(mask, spread)
    entry = jnp.broadcast_to(aperture[...].astype(jnp.float32), (8, 128)).astype(jnp.bfloat16)
    entry = dot(entry, spread)[:1].astype(jnp.int32)
    pick = one_hot(iota((256, 1024), 0) == entry)
    turns = phases[...]
    parts = []
    for value in (jnp.cos(turns), jnp.sin(turns)):
        for _ in range(3):
            piece = value.astype(jnp.bfloat16).astype(jnp.float32)
            parts.append(piece)
            value = value - piece
    parts = jnp.concatenate(parts + parts[:2], axis=0).astype(jnp.bfloat16)
    picked = dot(parts, pick)
    wc[...] = mask * (picked[0:1] + picked[1:2] + picked[2:3])
    ws[...] = mask * (picked[3:4] + picked[4:5] + picked[5:6])
    for rows, c_out, s_out in ((scan, ct, st), (scan ^ 1, ct2, st2)):
        row = rows * 32 + (iota((64, 128), 1) & 31)
        c1, s1 = turn(tile * 8 * row & 1023)
        row = rows * 32 + (iota((8, 128), 1) & 31)
        c2, s2 = turn(iota((8, 128), 0) * row & 1023)
        c1, s1 = c1[:, None, :], s1[:, None, :]
        c_out[...] = (c1 * c2[None] - s1 * s2[None]).reshape(512, 128)
        s_out[...] = -(s1 * c2[None] + c1 * s2[None]).reshape(512, 128)
    for piece, copy in zip(pieces, copies[3:]):
        copy.wait()
        f_high[piece, :], f_low[piece, :] = halves(frames[piece, :])

    def fill(step):
        tiles, rows = slice(step * 16, step * 16 + 16), slice(step * 128, step * 128 + 128)
        fill_matrix(wc[tiles, :], ws[tiles, :], ct[rows, :], st[rows, :], *matrices[2 * step - 2 : 2 * step])

    fill(1)
    for step in (1, 2, 3):
        if step < 3:
            fill(step + 1)
        high, low = matrices[2 * step - 2 : 2 * step]
        part[step * 256 : step * 256 + 256, :] = product(high, low, f_high, f_low)


def later_kernel(step, frames, part, wc, ws, ct, st, out, a_high, a_low, f_high, f_low):
    f_high[...], f_low[...] = halves(frames[...])
    tiles, rows = slice(step * 16, step * 16 + 16), slice(step * 128, step * 128 + 128)
    fill_matrix(wc[tiles, :], ws[tiles, :], ct[rows, :], st[rows, :], a_high, a_low)
    out[...] = part[step * 256 : step * 256 + 256, :] + product(a_high, a_low, f_high, f_low)


def near_kernel(own_high, own_low, frames, wc, ws, ct, st, ct2, st2, out, a_high, a_low, f_high, f_low):
    fill_matrix(wc[:16, :], ws[:16, :], ct[:128, :], st[:128, :], a_high, a_low)
    out[...] = product(a_high, a_low, own_high, own_low)
    f_high[...], f_low[...] = halves(frames[...])
    fill_matrix(wc[:16, :], ws[:16, :], ct2[:128, :], st2[:128, :], a_high, a_low)
    out[...] += product(a_high, a_low, f_high, f_low)


def add_kernel(a, b, out):
    out[...] = a[...] + b[...]


def split_kernel(a, b, *outs):
    rows = outs[0].shape[0]
    for step, out in enumerate(outs):
        at = slice(step * rows, step * rows + rows)
        out[...] = a[at, :] + b[at, :]


def sum_kernel(a, b, c, d, *outs):
    rows = outs[0].shape[0]
    for step, out in enumerate(outs):
        at = slice(step * rows, step * rows + rows)
        out[...] = a[at, :] + b[at, :] + c[at, :] + d[at, :]


def last_kernel(a, b, c, d, t_high, t_low, out):
    total = a[...] + b[...] + c[...] + d[...]
    columns = total.shape[1]
    high, low = halves(total)
    both = dot(jnp.concatenate([high, low], axis=0), t_high[...])
    both = both[:16] + both[16:] + dot(high, t_low[...])
    out[:, 0, :] = both[:8, :columns] + both[8:, columns:]
    out[:, 1, :] = both[8:, :columns] - both[:8, columns:]


def call(kernel, outs, scratch=(), flops=0, moved=0, inputs=0, limit=40 << 20):
    one = not isinstance(outs, (list, tuple))
    return pl.pallas_call(
        kernel,
        out_shape=outs,
        in_specs=[pl.BlockSpec(memory_space=pltpu.VMEM)] * inputs,
        out_specs=pl.BlockSpec(memory_space=pltpu.VMEM) if one else [pl.BlockSpec(memory_space=pltpu.VMEM)] * len(outs),
        scratch_shapes=list(scratch),
        cost_estimate=pl.CostEstimate(flops=flops, bytes_accessed=moved, transcendentals=0),
        compiler_params=pltpu.CompilerParams(vmem_limit_bytes=limit),
    )


def f32(*shape):
    return jax.ShapeDtypeStruct(shape, jnp.float32)


def bf16(*shape):
    return jax.ShapeDtypeStruct(shape, jnp.bfloat16)


def body(frames, intersection_masks, aperture, phases):
    col_len = frames.shape[2]
    where = jnp.stack([lax.axis_index("scan"), lax.axis_index("freq")]).astype(jnp.int32)
    swap = [(d, (d // 4 ^ 1) * 4 + d % 4) for d in range(128)]
    other = lax.ppermute(frames, AXES, swap).reshape(1024, col_len)
    vmem = pl.BlockSpec(memory_space=pltpu.VMEM)
    part, wc, ws, ct, st, ct2, st2, f_high, f_low = pl.pallas_call(
        own_kernel,
        out_shape=[f32(1024, col_len)] + [f32(64, 1024)] * 2 + [f32(512, 128)] * 4 + [bf16(1024, col_len)] * 2,
        in_specs=[pl.BlockSpec(memory_space=pltpu.SMEM)] + [pl.BlockSpec(memory_space=pltpu.HBM)] * 4,
        out_specs=[vmem] * 9,
        scratch_shapes=[
            pltpu.VMEM((1024, col_len), jnp.float32),
            pltpu.VMEM((128, 128), jnp.int32),
            pltpu.VMEM((1, 128), jnp.int32),
            pltpu.VMEM((1, 256), jnp.float32),
        ]
        + [pltpu.SemaphoreType.DMA((11,))]
        + [pltpu.VMEM((256, 1024), jnp.bfloat16)] * 6,
        cost_estimate=pl.CostEstimate(flops=6 * 768 * 1024 * 512, bytes_accessed=5 << 20, transcendentals=0),
        compiler_params=pltpu.CompilerParams(vmem_limit_bytes=24 << 20),
    )(where, *[pltpu.with_memory_space_constraint(u, pltpu.HBM) for u in (frames.reshape(1024, col_len), intersection_masks, aperture[None, :], phases[None, :])])

    scratch = [pltpu.VMEM((256, 1024), jnp.bfloat16)] * 2 + [pltpu.VMEM((1024, col_len), jnp.bfloat16)] * 2
    cost = dict(flops=1000, moved=1000, limit=24 << 20)
    block = f32(256, col_len)
    send = {
        step: call(functools.partial(later_kernel, step), block, scratch, inputs=6, **cost)(other, part, wc, ws, ct2, st2)
        for step in (3, 2, 1)
    }
    send[0] = call(near_kernel, block, scratch, inputs=9, **cost)(f_high, f_low, other, wc, ws, ct, st, ct2, st2)
    columns = np.arange(col_len)
    angle = 2.0 * np.pi / col_len * (columns[:, None] * columns[None, :] % col_len)
    scale = 1.0 / math.sqrt(1024 * col_len * 128)
    table = np.concatenate([np.cos(angle), np.sin(angle)], 1) * scale
    t_high = table.astype(jnp.bfloat16)
    t_low = (table - t_high.astype(np.float64)).astype(jnp.bfloat16)
    for step in (3, 2):
        got = lax.ppermute(send[step], AXES, partners(0, step - 1))
        send[0] = call(add_kernel, block, inputs=2, moved=3 << 19, limit=8 << 20)(send[0], got)
    got = lax.ppermute(send[1], AXES, partners(0, 0))
    send = call(split_kernel, [f32(64, col_len)] * 4, inputs=2, moved=3 << 19, limit=8 << 20)(send[0], got)
    got = [lax.ppermute(send[step], AXES, partners(1, step - 1)) for step in (3, 2, 1)]
    send = call(sum_kernel, [f32(16, col_len)] * 4, inputs=4, moved=5 << 17, limit=8 << 20)(send[0], *got)
    got = [lax.ppermute(send[step], AXES, partners(2, step - 1)) for step in (3, 2, 1)]
    return call(last_kernel, f32(8, 2, col_len), inputs=6, flops=1 << 26, moved=2 << 20, limit=8 << 20)(
        send[0], *got, jnp.asarray(t_high), jnp.asarray(t_low)
    )


def solution(mesh):
    in_specs = (P("freq", "scan", None), P(), P(), P())
    out_specs = P(("scan", "freq"), None, None)
    return jax.shard_map(body, mesh=mesh, in_specs=in_specs, out_specs=out_specs, check_vma=False)
```
